512 devices in a mesh: dp: 32 (over z, core), cent: 16 (over x, y).
Axes of the slice: x: 4, y: 4, z: 16, core: 2. Of those that a mesh axis runs over, the one named last changes fastest.
Arguments:
- embeddings: bfloat16 [262144, 1024], P(('dp', 'cent')), may hold values from -44.5 to 53.875
- centroids: float32 [131072, 1024], P(('dp', 'cent')), may hold values from -3 to 5
- candidates: int32 [1024, 8], P(('dp', 'cent')), may hold values from 0 to 15, all different within a row; in each aligned block of 32 rows (0 to 31, 32 to 63, ...) at most 24 rows name the same one
Outputs:
- new_centroids: float32 [131072, 1024], P(('dp', 'cent'))
- log_norm: float32 [262144], P(('dp', 'cent'))
- objective: float32 [], replicated
The draws below stay inside these ranges and needn't reach their ends.
Inputs may be any that keep to these rules, and one draw needn't show every extreme that they name: `candidates`: the 8 entries of a row block are different. Among the row blocks of one coarse group (aligned runs of 32 row blocks), no centroid block is named more than 24 times, and some centroid block is named exactly 24 times in every draw.
All inputs are finite; a program needn't handle non-finite values.
Results may differ from the reference program's by a relative error of at most 0.0067.
Values may be sent and summed in bfloat16 or wider, within the bound.
No kernel may reach another device: no remote copies, remote signals or barrier semaphores. Data moves between devices by JAX's collectives and lax.ppermute only.
A program may use at most 128 MiB of HBM per device.

```python
import math
import jax
import jax.numpy as jnp
import numpy as np
from jax import lax

D = 1024
BLK = 256
TOPC = 8
CB_DEV = 1
RB_DEV = 2
GROUP_BLOCKS = 16
MOST = 24
K = 131072
NRB = 1024
NROWS = 262144
N_DP = 32
N_CENT = 16


def centroid_noise(key):
    noise_key = jax.random.fold_in(key, 21)
    noise = jnp.clip(jax.random.normal(noise_key, (K, D), jnp.float32), -4.0, 4.0)
    return noise


def draw_centroids(key, part):
    return 1.0 + centroid_noise(key)


def draw_embeddings(key, part):
    noise_key = jax.random.fold_in(key, 11)
    pick_key = jax.random.fold_in(key, 12)
    level_key = jax.random.fold_in(key, 13)
    jitter_key = jax.random.fold_in(key, 14)
    partner_key = jax.random.fold_in(key, 15)
    strength_key = jax.random.fold_in(key, 16)
    noise = jnp.clip(jax.random.normal(noise_key, (NROWS, D), jnp.float32), -6.0, 6.0)
    group_size = RB_DEV * BLK * (GROUP_BLOCKS // CB_DEV)
    group_count = NROWS // group_size
    group_cents = GROUP_BLOCKS * BLK
    row_index = jnp.arange(NROWS, dtype=jnp.int32)
    group_of_row = row_index // group_size
    jitter = jax.random.randint(jitter_key, (group_count,), 0, 160)
    trend = 160 * jnp.arange(group_count, dtype=jnp.int32) // max(group_count - 1, 1)
    threshold = jitter + trend
    lifted = jax.random.randint(pick_key, (NROWS,), 0, 4096) < threshold[group_of_row]
    lifted = jnp.logical_or(lifted, row_index == 0)
    level = jax.random.uniform(level_key, (NROWS,), jnp.float32, 120.0, 320.0)
    offset = jnp.where(lifted, 0.5 + level / math.sqrt(D), 0.0)
    partner = group_of_row * group_cents + jax.random.randint(partner_key, (NROWS,), 0, group_cents)
    strength = jax.random.uniform(strength_key, (NROWS,), jnp.float32, 128.0, 288.0) / math.sqrt(D)
    strength = jnp.where(lifted, strength, 0.0)
    aligned = centroid_noise(key)[partner]
    return (noise + offset[:, None] + strength[:, None] * aligned).astype(jnp.bfloat16)


def shared_out(rng, own, number, rows, amount, top, most, slope):
    sequence = jax.random.permutation(rng, amount)
    crowded, common = load_shares(amount, rows * top, most, slope, True), load_shares(amount, rows * top, most, slope, False)
    places = jnp.arange(amount)

    def named(tallies, rotation):
        used = int((tallies > 0).sum())
        fixed = max(1, used // 4)
        moved = fixed + (places - fixed + rotation * (used - fixed)) % max(1, amount - fixed)
        return jnp.zeros((amount,), jnp.int32).at[sequence[jnp.where(places < fixed, places, moved)]].set(jnp.asarray(tallies, jnp.int32))

    tallies = jnp.where(number % 4 == 0, named(crowded, number // 4), named(common, number - number // 4 - 1))
    mixed = jax.random.permutation(jax.random.fold_in(own, 3), amount)
    donor, receiver = mixed[0:amount // 2 * 2:2], mixed[1:amount // 2 * 2:2]
    margin = jnp.minimum(tallies[donor] - 1, most - tallies[receiver]) // 2
    margin = jnp.where((donor == sequence[0]) | (receiver == sequence[0]) | (tallies[receiver] == 0), 0, jnp.maximum(margin, 0))
    moved = jax.random.randint(jax.random.fold_in(own, 4), (amount // 2,), 0, 1 << 20) % (margin + 1)
    tallies = tallies.at[donor].add(-moved).at[receiver].add(moved)
    items = jnp.searchsorted(jnp.cumsum(tallies), jnp.arange(rows * top), side="right").astype(jnp.int32)
    grid = items.reshape(top, rows).T
    grid = grid[jax.random.permutation(jax.random.fold_in(own, 1), rows)]
    rotation = jax.random.randint(jax.random.fold_in(own, 2), (rows, 1), 0, top)
    return jnp.take_along_axis(grid, (jnp.arange(top)[None, :] + rotation) % top, axis=1)


def load_shares(number_of, total, most, lean, full):
    portions = [(1 << 20) // math.isqrt(grade ** lean) + 1 for grade in range(1, number_of + 1)]
    largest = most if full else min(most, max(-(-total // number_of), total * portions[0] // sum(portions)))
    least = 1 if total - largest >= number_of - 1 else 0
    holding, spare = [largest] + [least] * (number_of - 1), total - largest - least * (number_of - 1)
    while spare > 0:
        free = [i for i in range(1, number_of) if holding[i] < largest] or [i for i in range(1, number_of) if holding[i] < most]
        whole, budget = sum([portions[i] for i in free]), spare
        for i in free:
            more = min(most - holding[i], max(1, budget * portions[i] // whole), spare)
            holding[i] = holding[i] + more
            spare = spare - more
    return np.array(holding)


def setup_inputs(seed: int = 0) -> dict:
    key_of = jax.random.split(jax.random.key(seed), 4)
    embeddings = draw_embeddings(jax.random.fold_in(key_of[3], 71), 0)
    centroids = draw_centroids(jax.random.fold_in(key_of[3], 71), 0)
    candidates_keys = jax.random.split(jax.random.fold_in(key_of[2], 1), NRB // (RB_DEV * N_CENT))
    candidates_turns = jax.random.permutation(jax.random.fold_in(key_of[2], 3), NRB // (RB_DEV * N_CENT))
    candidates = jax.vmap(lambda own, number: shared_out(jax.random.fold_in(key_of[2], 2), own, number, RB_DEV * N_CENT, CB_DEV * N_CENT, TOPC, MOST, 2))(candidates_keys, candidates_turns).reshape((NRB, TOPC))
    return {"embeddings": embeddings, "centroids": centroids, "candidates": candidates}


def group_update(group_rows, group_cents, group_lists):
    cent_bf = lax.optimization_barrier(group_cents.astype(jnp.bfloat16))
    half_norm = 0.5 * lax.optimization_barrier(jnp.sum(group_cents * group_cents, axis=2))

    def row_step(carry, inputs):
        block_sums, block_counts = carry
        row_block, id_list = inputs
        chosen = cent_bf[id_list].astype(jnp.float32)
        row_values = row_block.astype(jnp.float32)
        dot_scores = jnp.einsum('bd,tkd->btk', row_values, chosen, precision=lax.Precision.HIGHEST)
        logits = (dot_scores - half_norm[id_list][None]) / math.sqrt(D)
        peak_value = lax.optimization_barrier(jnp.max(logits, axis=(1, 2)))
        row_log = peak_value + jnp.log(lax.optimization_barrier(jnp.sum(jnp.exp(logits - peak_value[:, None, None]), axis=(1, 2))))
        weights = jnp.exp(logits - row_log[:, None, None])
        block_counts = block_counts.at[id_list].add(lax.optimization_barrier(jnp.sum(weights, axis=0)))
        weights_bf = lax.optimization_barrier(weights.astype(jnp.bfloat16)).astype(jnp.float32)
        block_terms = jnp.einsum('btk,bd->tkd', weights_bf, row_values, precision=lax.Precision.HIGHEST)
        block_sums = block_sums.at[id_list].add(block_terms)
        return ((block_sums, block_counts), row_log)
    zero_sums = jnp.zeros(group_cents.shape, jnp.float32)
    zero_counts = jnp.zeros(group_cents.shape[:2], jnp.float32)
    (block_sums, block_counts), row_logs = lax.scan(row_step, (zero_sums, zero_counts), (group_rows, group_lists))
    new_cents = (block_sums + group_cents) / (block_counts[..., None] + 1.0)
    return (new_cents, row_logs)

def group_apply(inputs):
    return group_update(inputs[0], inputs[1], inputs[2])

def reference(embeddings, centroids, candidates):
    row_groups = embeddings.reshape(N_DP, RB_DEV * N_CENT, BLK, D)
    cent_groups = centroids.reshape(N_DP, GROUP_BLOCKS, BLK, D)
    list_groups = candidates.reshape(N_DP, RB_DEV * N_CENT, TOPC)
    new_cents, row_logs = lax.map(group_apply, (row_groups, cent_groups, list_groups))
    log_norm = row_logs.reshape(NROWS)
    objective = jnp.sum(log_norm) / NROWS
    return (new_cents.reshape(K, D), log_norm, objective)
```

```python
import functools

import jax
import jax.numpy as jnp
from jax import lax
from jax.experimental import pallas as pl
from jax.experimental.pallas import tpu as pltpu
from jax.sharding import PartitionSpec as P

BLK = 256
SIDE = 4
CORES = 2
PAD = 128
AXES = ("dp", "cent")
SHIFTS = (0, 1, 3, 2)
FLOOR = -1e30


def device_at(plane, core, x, y):
    return (plane * CORES + core) * SIDE * SIDE + x * SIDE + y


def line_device(plane, core, row_pos, cent_pos):
    if core == 0:
        return device_at(plane, core, row_pos, cent_pos)
    return device_at(plane, core, cent_pos, row_pos)


def row_pairs(planes, shift):
    return [
        (line_device(z, c, (r + shift) % SIDE, k), line_device(z, c, r, k))
        for z in range(planes)
        for c in range(CORES)
        for r in range(SIDE)
        for k in range(SIDE)
    ]


def cent_pairs(planes, shift):
    return [
        (line_device(z, c, r, (k + shift) % SIDE), line_device(z, c, r, k))
        for z in range(planes)
        for c in range(CORES)
        for r in range(SIDE)
        for k in range(SIDE)
    ]


def row_lines(planes):
    return [
        [line_device(z, c, r, k) for r in range(SIDE)]
        for z in range(planes)
        for c in range(CORES)
        for k in range(SIDE)
    ]


def line_covers(planes):
    return [
        [line_device(z, c, r, k) for c in range(CORES) for z in range(planes) for k in range(SIDE)]
        for r in range(SIDE)
    ]


def split3(value):
    high = value.astype(jnp.bfloat16)
    rest = value - high.astype(jnp.float32)
    middle = rest.astype(jnp.bfloat16)
    low = (rest - middle.astype(jnp.float32)).astype(jnp.bfloat16)
    return high, middle, low


def tail_lanes(value):
    high, middle, low = (part.astype(jnp.float32) for part in split3(value))
    lane = lax.broadcasted_iota(jnp.int32, (value.shape[0], PAD), 1)
    tail = jnp.where(lane == 0, high, jnp.where(lane == 1, middle, jnp.where(lane == 2, low, 0.0)))
    return tail.astype(jnp.bfloat16)


def read_tail(ref, width):
    tail = ref[:, width:].astype(jnp.float32)
    return tail[:, 0:1] + tail[:, 1:2] + tail[:, 2:3]


def pack_kernel(cent_ref, out_ref):
    width = cent_ref.shape[1]
    values = cent_ref[...]
    out_ref[:, :width] = values.astype(jnp.bfloat16)
    out_ref[:, width:] = tail_lanes(0.5 * jnp.sum(values * values, axis=1, keepdims=True))


def score_kernel(scale, extra, row_ref, *refs):
    cents = refs[:SIDE]
    before = refs[SIDE : SIDE + extra]
    exps = refs[SIDE + extra : 2 * SIDE + extra]
    stat_ref = refs[2 * SIDE + extra]
    width = row_ref.shape[1]
    base = 0
    for ref in before:
        stat_ref[base : base + ref.shape[0], :] = ref[...]
        base += ref.shape[0]
    for j in range(SIDE):
        dots = lax.dot_general(
            cents[j][:, :width],
            row_ref[...],
            (((1,), (1,)), ((), ())),
            preferred_element_type=jnp.float32,
        )
        logits = (dots - read_tail(cents[j], width)) * scale
        peak = jnp.max(logits, axis=0, keepdims=True)
        exp_values = jnp.exp(logits - peak)
        exps[j][...] = exp_values
        stat_ref[base + j : base + j + 1, :] = peak
        stat_ref[base + SIDE + j : base + SIDE + j + 1, :] = jnp.sum(
            exp_values, axis=0, keepdims=True
        )


def norm_kernel(pos_ref, all_ref, own_ref, scale_ref, log_ref, sum_ref):
    me = pos_ref[0]
    allow_base = 2 * SIDE

    def allowed(r):
        return all_ref[r, 0 : SIDE * SIDE, :]

    def stat_rows(ref, index):
        start = SIDE * SIDE + index * allow_base
        return ref[start : start + SIDE, :], ref[start + SIDE : start + 2 * SIDE, :]

    logs = []
    for r in range(SIDE):
        allow = allowed(r)
        peaks, totals = [], []
        for q in range(SIDE):
            peak, total = stat_rows(all_ref.at[q], SHIFTS.index((r - q) % SIDE))
            peaks.append(peak)
            totals.append(total)
        peak = jnp.concatenate(peaks, axis=0)
        total = jnp.concatenate(totals, axis=0)
        top = jnp.max(jnp.where(allow > 0, peak, FLOOR), axis=0, keepdims=True)
        parts = jnp.where(allow > 0, total * jnp.exp(jnp.minimum(peak - top, 0.0)), 0.0)
        logs.append(top + jnp.log(jnp.sum(parts, axis=0, keepdims=True)))
    row_sum = logs[0] + logs[1] + logs[2] + logs[3]
    sum_ref[...] = jnp.broadcast_to(jnp.sum(row_sum, axis=1, keepdims=True), sum_ref.shape)
    for t in range(SIDE):
        place = lax.rem(me + SHIFTS[t], SIDE)
        log_t = jnp.zeros_like(logs[0])
        allow_t = jnp.zeros((SIDE, log_t.shape[1]), jnp.float32)
        for r in range(SIDE):
            here = place == r
            log_t = jnp.where(here, logs[r], log_t)
            for q in range(SIDE):
                allow_t = jnp.where(
                    jnp.logical_and(here, me == q), allowed(r)[q * SIDE : (q + 1) * SIDE, :], allow_t
                )
        peak, _ = stat_rows(own_ref, t)
        scale_ref[t * SIDE : (t + 1) * SIDE, :] = jnp.where(
            allow_t > 0, jnp.exp(jnp.minimum(peak - log_t, 0.0)), 0.0
        )
        if t == 0:
            log_ref[...] = log_t


def weighted(j, scale_ref, exps, rows):
    total, lanes = None, None
    for t in range(SIDE):
        weights = exps[t][...] * scale_ref[t * SIDE + j : t * SIDE + j + 1, :]
        for start in range(0, weights.shape[1], PAD):
            piece = weights[:, start : start + PAD]
            lanes = piece if lanes is None else lanes + piece
        term = jnp.dot(
            weights.astype(jnp.bfloat16), rows[t][...], preferred_element_type=jnp.float32
        )
        total = term if total is None else total + term
    return total, jnp.sum(lanes, axis=1, keepdims=True)


def send_kernel(j, scale_ref, *refs):
    exps, rows, out_ref = refs[:SIDE], refs[SIDE : 2 * SIDE], refs[2 * SIDE]
    width = rows[0].shape[1]
    total, counts = weighted(j, scale_ref, exps, rows)
    out_ref[:, :width] = total.astype(jnp.bfloat16)
    out_ref[:, width:] = tail_lanes(counts)


def keep_kernel(j, scale_ref, *refs):
    exps, rows = refs[:SIDE], refs[SIDE : 2 * SIDE]
    total_ref, count_ref = refs[2 * SIDE :]
    total, counts = weighted(j, scale_ref, exps, rows)
    total_ref[...] = total
    count_ref[...] = jnp.broadcast_to(counts, count_ref.shape)


def final_kernel(total_ref, count_ref, a_ref, b_ref, c_ref, old_ref, out_ref):
    width = total_ref.shape[1]
    total = total_ref[...] + old_ref[...]
    counts = count_ref[:, 0:1] + 1.0
    for ref in (a_ref, b_ref, c_ref):
        total = total + ref[:, :width].astype(jnp.float32)
        counts = counts + read_tail(ref, width)
    out_ref[...] = total / counts


def call(kernel, name, outs, n_in, flops=0, nbytes=0, smem_first=False):
    vmem = pl.BlockSpec(memory_space=pltpu.VMEM)
    smem = pl.BlockSpec(memory_space=pltpu.SMEM)
    in_specs = [smem if smem_first and i == 0 else vmem for i in range(n_in)]
    return pl.pallas_call(
        kernel,
        name=name,
        out_shape=outs,
        in_specs=in_specs,
        out_specs=jax.tree.map(lambda _: vmem, outs),
        cost_estimate=pl.CostEstimate(flops=flops, bytes_accessed=nbytes, transcendentals=0),
        compiler_params=pltpu.CompilerParams(vmem_limit_bytes=48 * 1024 * 1024),
    )


def per_device(embeddings, centroids, candidates):
    planes = lax.axis_size("dp") // CORES
    core = lax.axis_index("dp") % CORES
    cent_index = lax.axis_index("cent")
    x, y = cent_index // SIDE, cent_index % SIDE
    row_pos = jnp.where(core == 0, x, y)
    cent_pos = jnp.where(core == 0, y, x)
    row_len, width = embeddings.shape
    own_row_blocks = candidates.shape[0]
    f32, bf16 = jnp.float32, jnp.bfloat16
    shape = jax.ShapeDtypeStruct

    rows = [embeddings] + [
        lax.ppermute(embeddings, AXES, row_pairs(planes, shift)) for shift in SHIFTS[1:]
    ]
    packed = call(pack_kernel, "pack", shape((BLK, width + PAD), bf16), 1, nbytes=2 << 20)(centroids)
    cents = [packed] + [
        lax.ppermute(packed, AXES, cent_pairs(planes, shift)) for shift in SHIFTS[1:]
    ]

    line = jnp.arange(SIDE, dtype=jnp.int32)
    other = (cent_pos + jnp.array(SHIFTS, jnp.int32)) % SIDE
    ids = jnp.where(
        core == 0, line[:, None] * SIDE + other[None, :], other[None, :] * SIDE + line[:, None]
    ).reshape(-1)
    allow = jnp.any(candidates[None] == ids[:, None, None], axis=2).astype(f32)
    allow = jnp.broadcast_to(
        allow[:, :, None], (SIDE * SIDE, own_row_blocks, row_len // own_row_blocks)
    ).reshape(SIDE * SIDE, row_len)

    exps, stats = [], [allow]
    pair_flops = 2 * row_len * SIDE * BLK * width
    for t in range(SIDE):
        extra = stats if t == SIDE - 1 else []
        stat_rows = 2 * SIDE + sum(s.shape[0] for s in extra)
        outs = [shape((BLK, row_len), f32)] * SIDE + [shape((stat_rows, row_len), f32)]
        *exp_values, stat = call(
            functools.partial(score_kernel, 1.0 / width**0.5, len(extra)),
            "score",
            outs,
            1 + SIDE + len(extra),
            flops=pair_flops,
            nbytes=6 << 20,
        )(rows[t], *cents, *extra)
        exps.append(exp_values)
        stats.append(stat)
    own_stats = stats[-1]
    all_stats = lax.all_gather(own_stats, AXES, axis_index_groups=row_lines(planes))
    n_cover = planes * CORES * SIDE
    scale, log_rows, line_sum = call(
        norm_kernel,
        "norm",
        [shape((SIDE * SIDE, row_len), f32), shape((1, row_len), f32), shape((n_cover, PAD), f32)],
        3,
        nbytes=1 << 20,
        smem_first=True,
    )(row_pos.reshape(1).astype(jnp.int32), all_stats, own_stats)

    received = []
    for j in (3, 1, 2):
        sent = call(
            functools.partial(send_kernel, j),
            "send",
            shape((BLK, width + PAD), bf16),
            1 + 2 * SIDE,
            flops=pair_flops,
            nbytes=6 << 20,
        )(scale, *[exps[t][j] for t in range(SIDE)], *rows)
        back = (SIDE - SHIFTS[j]) % SIDE
        received.append(lax.ppermute(sent, AXES, cent_pairs(planes, back)))
    total, counts = call(
        functools.partial(keep_kernel, 0),
        "keep",
        [shape((BLK, width), f32), shape((BLK, PAD), f32)],
        1 + 2 * SIDE,
        flops=pair_flops,
        nbytes=6 << 20,
    )(scale, *[exps[t][0] for t in range(SIDE)], *rows)
    cover_sums = lax.all_to_all(
        line_sum, AXES, 0, 0, tiled=True, axis_index_groups=line_covers(planes)
    )
    n_rows = row_len * lax.axis_size("dp") * SIDE * SIDE
    objective = jnp.sum(cover_sums[:, 0]) / n_rows
    new_centroids = call(final_kernel, "final", shape((BLK, width), f32), 6, nbytes=5 << 20)(
        total, counts, *received, centroids
    )
    return new_centroids, log_rows.reshape(row_len), objective


def solution(mesh):
    in_specs = (P(AXES, None), P(AXES, None), P(AXES, None))
    out_specs = (P(AXES, None), P(AXES), P())
    return jax.shard_map(
        per_device, mesh=mesh, in_specs=in_specs, out_specs=out_specs, check_vma=False
    )
```

```python
import functools

import jax
import jax.numpy as jnp
from jax import lax
from jax.experimental import pallas as pl
from jax.experimental.pallas import tpu as pltpu
from jax.sharding import PartitionSpec as P


BLK = 256
SIDE = 4
CORES = 2
PAD = 128
AXES = ("dp", "cent")
SHIFTS = (0, 1, 3, 2)
FLOOR = -1e30


def device_at(plane, core, x, y):
    return (plane * CORES + core) * SIDE * SIDE + x * SIDE + y


def line_device(plane, core, row_pos, cent_pos):
    if core == 0:
        return device_at(plane, core, row_pos, cent_pos)
    return device_at(plane, core, cent_pos, row_pos)


def row_pairs(planes, shift):
    return [
        (line_device(z, c, (r + shift) % SIDE, k), line_device(z, c, r, k))
        for z in range(planes)
        for c in range(CORES)
        for r in range(SIDE)
        for k in range(SIDE)
    ]


def cent_pairs(planes, shift):
    return [
        (line_device(z, c, r, (k + shift) % SIDE), line_device(z, c, r, k))
        for z in range(planes)
        for c in range(CORES)
        for r in range(SIDE)
        for k in range(SIDE)
    ]


def row_lines(planes):
    return [
        [line_device(z, c, r, k) for r in range(SIDE)]
        for z in range(planes)
        for c in range(CORES)
        for k in range(SIDE)
    ]


def line_covers(planes):
    return [
        [line_device(z, c, r, k) for c in range(CORES) for z in range(planes) for k in range(SIDE)]
        for r in range(SIDE)
    ]


def split3(value):
    high = value.astype(jnp.bfloat16)
    rest = value - high.astype(jnp.float32)
    middle = rest.astype(jnp.bfloat16)
    low = (rest - middle.astype(jnp.float32)).astype(jnp.bfloat16)
    return high, middle, low


def tail_lanes(value):
    high, middle, low = (part.astype(jnp.float32) for part in split3(value))
    lane = lax.broadcasted_iota(jnp.int32, (value.shape[0], PAD), 1)
    tail = jnp.where(lane == 0, high, jnp.where(lane == 1, middle, jnp.where(lane == 2, low, 0.0)))
    return tail.astype(jnp.bfloat16)


def read_tail(ref, width):
    tail = ref[:, width:].astype(jnp.float32)
    return tail[:, 0:1] + tail[:, 1:2] + tail[:, 2:3]


def pack_kernel(cent_ref, out_ref):
    width = cent_ref.shape[1]
    values = cent_ref[...]
    out_ref[:, :width] = values.astype(jnp.bfloat16)
    out_ref[:, width:] = tail_lanes(0.5 * jnp.sum(values * values, axis=1, keepdims=True))


def score_kernel(scale, n_rows, extra, *refs):
    rows, cents = refs[:n_rows], refs[n_rows : n_rows + SIDE]
    before = refs[n_rows + SIDE : n_rows + SIDE + extra]
    exps = refs[n_rows + SIDE + extra : n_rows + 2 * SIDE + extra]
    stat_ref = refs[n_rows + 2 * SIDE + extra]
    width = rows[0].shape[1]
    base = 0
    for ref in before:
        stat_ref[base : base + ref.shape[0], :] = ref[...]
        base += ref.shape[0]
    for j in range(SIDE):
        half = read_tail(cents[j], width)
        start = 0
        for row_ref in rows:
            stop = start + row_ref.shape[0]
            dots = lax.dot_general(
                cents[j][:, :width],
                row_ref[...],
                (((1,), (1,)), ((), ())),
                preferred_element_type=jnp.float32,
            )
            logits = (dots - half) * scale
            peak = jnp.max(logits, axis=0, keepdims=True)
            exp_values = jnp.exp(logits - peak)
            exps[j][:, start:stop] = exp_values
            stat_ref[base + j : base + j + 1, start:stop] = peak
            stat_ref[base + SIDE + j : base + SIDE + j + 1, start:stop] = jnp.sum(
                exp_values, axis=0, keepdims=True
            )
            start = stop


def norm_kernel(pos_ref, all_ref, own_ref, scale_ref, log_ref, sum_ref):
    me = pos_ref[0]
    allow_base = 2 * SIDE

    def allowed(r):
        return all_ref[r, 0 : SIDE * SIDE, :]

    def stat_rows(ref, index):
        start = SIDE * SIDE + index * allow_base
        return ref[start : start + SIDE, :], ref[start + SIDE : start + 2 * SIDE, :]

    logs = []
    for r in range(SIDE):
        allow = allowed(r)
        peaks, totals = [], []
        for q in range(SIDE):
            peak, total = stat_rows(all_ref.at[q], SHIFTS.index((r - q) % SIDE))
            peaks.append(peak)
            totals.append(total)
        peak = jnp.concatenate(peaks, axis=0)
        total = jnp.concatenate(totals, axis=0)
        top = jnp.max(jnp.where(allow > 0, peak, FLOOR), axis=0, keepdims=True)
        parts = jnp.where(allow > 0, total * jnp.exp(jnp.minimum(peak - top, 0.0)), 0.0)
        logs.append(top + jnp.log(jnp.sum(parts, axis=0, keepdims=True)))
    row_sum = logs[0] + logs[1] + logs[2] + logs[3]
    sum_ref[...] = jnp.broadcast_to(jnp.sum(row_sum, axis=1, keepdims=True), sum_ref.shape)
    for t in range(SIDE):
        place = lax.rem(me + SHIFTS[t], SIDE)
        log_t = jnp.zeros_like(logs[0])
        allow_t = jnp.zeros((SIDE, log_t.shape[1]), jnp.float32)
        for r in range(SIDE):
            here = place == r
            log_t = jnp.where(here, logs[r], log_t)
            for q in range(SIDE):
                allow_t = jnp.where(
                    jnp.logical_and(here, me == q), allowed(r)[q * SIDE : (q + 1) * SIDE, :], allow_t
                )
        peak, _ = stat_rows(own_ref, t)
        scale_ref[t * SIDE : (t + 1) * SIDE, :] = jnp.where(
            allow_t > 0, jnp.exp(jnp.minimum(peak - log_t, 0.0)), 0.0
        )
        if t == 0:
            log_ref[...] = log_t


def weighted(j, scale_ref, exps, rows):
    total, lanes = None, None
    for t in range(SIDE):
        weights = exps[t][...] * scale_ref[t * SIDE + j : t * SIDE + j + 1, :]
        for start in range(0, weights.shape[1], PAD):
            piece = weights[:, start : start + PAD]
            lanes = piece if lanes is None else lanes + piece
        rounded = weights.astype(jnp.bfloat16)
        start = 0
        for row_ref in rows[t]:
            stop = start + row_ref.shape[0]
            term = jnp.dot(
                rounded[:, start:stop], row_ref[...], preferred_element_type=jnp.float32
            )
            total = term if total is None else total + term
            start = stop
    return total, jnp.sum(lanes, axis=1, keepdims=True)


def sums_kernel(scale_ref, *refs):
    n_rows = SIDE + 1
    flat, row_refs = refs[: SIDE * SIDE], refs[SIDE * SIDE : SIDE * SIDE + n_rows]
    outs = refs[SIDE * SIDE + n_rows :]
    rows = [[row_refs[0]], [row_refs[1]], [row_refs[2]], [row_refs[3], row_refs[4]]]
    width = row_refs[0].shape[1]
    for j in range(SIDE - 1, -1, -1):
        exps = [flat[t * SIDE + j] for t in range(SIDE)]
        total, counts = weighted(j, scale_ref, exps, rows)
        if j == 0:
            outs[0][...] = total
            outs[SIDE][...] = jnp.broadcast_to(counts, outs[SIDE].shape)
        else:
            outs[j][:, :width] = total.astype(jnp.bfloat16)
            outs[j][:, width:] = tail_lanes(counts)


def final_kernel(total_ref, count_ref, a_ref, b_ref, c_ref, old_ref, out_ref):
    width = total_ref.shape[1]
    total = total_ref[...] + old_ref[...]
    counts = count_ref[:, 0:1] + 1.0
    for ref in (a_ref, b_ref, c_ref):
        total = total + ref[:, :width].astype(jnp.float32)
        counts = counts + read_tail(ref, width)
    out_ref[...] = total / counts


def call(kernel, outs, n_in, limit, flops=0, nbytes=0, smem_first=False):
    vmem = pl.BlockSpec(memory_space=pltpu.VMEM)
    smem = pl.BlockSpec(memory_space=pltpu.SMEM)
    in_specs = [smem if smem_first and i == 0 else vmem for i in range(n_in)]
    return pl.pallas_call(
        kernel,
        out_shape=outs,
        in_specs=in_specs,
        out_specs=jax.tree.map(lambda _: vmem, outs),
        cost_estimate=pl.CostEstimate(flops=flops, bytes_accessed=nbytes, transcendentals=0),
        compiler_params=pltpu.CompilerParams(vmem_limit_bytes=limit << 20),
    )


def bulk(value, pairs):
    return lax.ppermute(value, AXES, pairs)


def step(embeddings, centroids, candidates):
    planes = lax.axis_size("dp") // CORES
    core = lax.axis_index("dp") % CORES
    cent_index = lax.axis_index("cent")
    x, y = cent_index // SIDE, cent_index % SIDE
    row_pos = jnp.where(core == 0, x, y)
    cent_pos = jnp.where(core == 0, y, x)
    row_len, width = embeddings.shape
    f32, bf16 = jnp.float32, jnp.bfloat16
    shape = jax.ShapeDtypeStruct

    packed = call(pack_kernel, shape((BLK, width + PAD), bf16), 1, 8, nbytes=2 << 20)(centroids)
    cents = [packed] + [bulk(packed, cent_pairs(planes, SHIFTS[t])) for t in range(1, SIDE)]
    near = bulk(embeddings, row_pairs(planes, 1))
    back = bulk(embeddings, row_pairs(planes, SIDE - 1))
    half = row_len // 2
    far = [bulk(near[:half], row_pairs(planes, 1)), bulk(back[half:], row_pairs(planes, SIDE - 1))]
    rows = [[embeddings], [near], [back], far]

    line = jnp.arange(SIDE, dtype=jnp.int32)
    other = (cent_pos + jnp.array(SHIFTS, jnp.int32)) % SIDE
    ids = jnp.where(
        core == 0, line[:, None] * SIDE + other[None, :], other[None, :] * SIDE + line[:, None]
    ).reshape(-1)
    allow = jnp.any(candidates[None] == ids[:, None, None], axis=2).astype(f32)
    allow = jnp.broadcast_to(
        allow[:, :, None], (SIDE * SIDE, candidates.shape[0], row_len // candidates.shape[0])
    ).reshape(SIDE * SIDE, row_len)

    exps, stats = [], [allow]
    pair_flops = 2 * row_len * SIDE * BLK * width
    for t in range(SIDE):
        extra = stats if t == SIDE - 1 else []
        stat_rows = 2 * SIDE + sum(part.shape[0] for part in extra)
        *exp_values, stat = call(
            functools.partial(score_kernel, 1.0 / width**0.5, len(rows[t]), len(extra)),
            [shape((BLK, row_len), f32)] * SIDE + [shape((stat_rows, row_len), f32)],
            len(rows[t]) + SIDE + len(extra),
            12,
            flops=pair_flops,
            nbytes=6 << 20,
        )(*rows[t], *cents, *extra)
        exps.append(exp_values)
        stats.append(stat)
    own_stats = stats[-1]
    all_stats = lax.all_gather(own_stats, AXES, axis_index_groups=row_lines(planes))
    n_cover = planes * CORES * SIDE
    scale, log_rows, line_sum = call(
        norm_kernel,
        [shape((SIDE * SIDE, row_len), f32), shape((1, row_len), f32), shape((n_cover, PAD), f32)],
        3,
        4,
        nbytes=1 << 20,
        smem_first=True,
    )(row_pos.reshape(1).astype(jnp.int32), all_stats, own_stats)

    total, *sent, counts = call(
        sums_kernel,
        [shape((BLK, width), f32)]
        + [shape((BLK, width + PAD), bf16)] * (SIDE - 1)
        + [shape((BLK, PAD), f32)],
        2 + SIDE * SIDE + SIDE,
        24,
        flops=SIDE * pair_flops,
        nbytes=16 << 20,
    )(scale, *[value for values in exps for value in values], *[part for parts in rows for part in parts])
    line_sum, sent, total, counts = lax.optimization_barrier((line_sum, sent, total, counts))
    cover_sums = lax.all_to_all(
        line_sum, AXES, 0, 0, tiled=True, axis_index_groups=line_covers(planes)
    )
    received = [bulk(sent[j - 1], cent_pairs(planes, -SHIFTS[j] % SIDE)) for j in (3, 1, 2)]
    tile = BLK // 2
    spec = lambda cols: pl.BlockSpec((tile, cols), lambda i: (i, 0))
    new_centroids = pl.pallas_call(
        final_kernel,
        name="final",
        grid=(BLK // tile,),
        out_shape=shape((BLK, width), f32),
        in_specs=[spec(width), spec(PAD)] + [spec(width + PAD)] * 3 + [spec(width)],
        out_specs=spec(width),
        cost_estimate=pl.CostEstimate(flops=0, bytes_accessed=5 << 20, transcendentals=0),
        compiler_params=pltpu.CompilerParams(vmem_limit_bytes=8 << 20),
    )(total, counts, *received, centroids)
    n_rows = row_len * lax.axis_size("dp") * SIDE * SIDE
    new_centroids, cover_sums = lax.optimization_barrier((new_centroids, cover_sums))
    objective = jnp.sum(cover_sums[:, 0]) / n_rows
    return new_centroids, log_rows.reshape(row_len), objective


def solution(mesh):
    in_specs = (P(AXES, None), P(AXES, None), P(AXES, None))
    out_specs = (P(AXES, None), P(AXES), P())
    return jax.shard_map(step, mesh=mesh, in_specs=in_specs, out_specs=out_specs, check_vma=False)
```

```python
import functools

import jax
import jax.numpy as jnp
from jax import lax
from jax.experimental import pallas as pl
from jax.experimental.pallas import tpu as pltpu
from jax.sharding import PartitionSpec as P


BLK = 256
SIDE = 4
CORES = 2
PAD = 128
AXES = ("dp", "cent")
SHIFTS = (0, 1, 3, 2)
FLOOR = -1e30


def device_at(plane, core, x, y):
    return (plane * CORES + core) * SIDE * SIDE + x * SIDE + y


def line_device(plane, core, row_pos, cent_pos):
    if core == 0:
        return device_at(plane, core, row_pos, cent_pos)
    return device_at(plane, core, cent_pos, row_pos)


def row_pairs(planes, shift):
    return [
        (line_device(z, c, (r + shift) % SIDE, k), line_device(z, c, r, k))
        for z in range(planes)
        for c in range(CORES)
        for r in range(SIDE)
        for k in range(SIDE)
    ]


def cent_pairs(planes, shift):
    return [
        (line_device(z, c, r, (k + shift) % SIDE), line_device(z, c, r, k))
        for z in range(planes)
        for c in range(CORES)
        for r in range(SIDE)
        for k in range(SIDE)
    ]


def row_lines(planes):
    return [
        [line_device(z, c, r, k) for r in range(SIDE)]
        for z in range(planes)
        for c in range(CORES)
        for k in range(SIDE)
    ]


def line_covers(planes):
    return [
        [line_device(z, c, r, k) for c in range(CORES) for z in range(planes) for k in range(SIDE)]
        for r in range(SIDE)
    ]


def split3(value):
    high = value.astype(jnp.bfloat16)
    rest = value - high.astype(jnp.float32)
    middle = rest.astype(jnp.bfloat16)
    low = (rest - middle.astype(jnp.float32)).astype(jnp.bfloat16)
    return high, middle, low


def tail_lanes(value):
    high, middle, low = (part.astype(jnp.float32) for part in split3(value))
    lane = lax.broadcasted_iota(jnp.int32, (value.shape[0], PAD), 1)
    tail = jnp.where(lane == 0, high, jnp.where(lane == 1, middle, jnp.where(lane == 2, low, 0.0)))
    return tail.astype(jnp.bfloat16)


def read_tail(ref, width):
    tail = ref[:, width:].astype(jnp.float32)
    return tail[:, 0:1] + tail[:, 1:2] + tail[:, 2:3]


def pack_kernel(cent_ref, out_ref):
    width = cent_ref.shape[1]
    values = cent_ref[...]
    out_ref[:, :width] = values.astype(jnp.bfloat16)
    out_ref[:, width:] = tail_lanes(0.5 * jnp.sum(values * values, axis=1, keepdims=True))


def allow_rows(pos_ref, list_ref, stat_ref):
    core, cent_pos = pos_ref[1], pos_ref[2]
    row_len = stat_ref.shape[1]
    second = lax.broadcasted_iota(jnp.int32, (1, row_len), 1) >= row_len // 2
    for q in range(SIDE):
        for j in range(SIDE):
            other = lax.rem(cent_pos + SHIFTS[j], SIDE)
            block = jnp.where(core == 0, q * SIDE + other, other * SIDE + q)
            hits = []
            for b in range(list_ref.shape[0]):
                hit = list_ref[b, 0] == block
                for i in range(1, list_ref.shape[1]):
                    hit = jnp.logical_or(hit, list_ref[b, i] == block)
                hits.append(jnp.where(hit, 1.0, 0.0))
            stat_ref[q * SIDE + j : q * SIDE + j + 1, :] = jnp.where(second, hits[1], hits[0])


def first_score_kernel(scale, pos_ref, list_ref, *refs):
    allow_rows(pos_ref, list_ref, refs[-1])
    score_kernel(scale, 1, 0, *refs, base=SIDE * SIDE)


def score_kernel(scale, n_rows, extra, *refs, base=0):
    rows, cents = refs[:n_rows], refs[n_rows : n_rows + SIDE]
    before = refs[n_rows + SIDE : n_rows + SIDE + extra]
    exps = refs[n_rows + SIDE + extra : n_rows + 2 * SIDE + extra]
    stat_ref = refs[n_rows + 2 * SIDE + extra]
    width = rows[0].shape[1]
    for ref in before:
        stat_ref[base : base + ref.shape[0], :] = ref[...]
        base += ref.shape[0]
    for j in range(SIDE):
        half = read_tail(cents[j], width)
        start = 0
        for row_ref in rows:
            stop = start + row_ref.shape[0]
            dots = lax.dot_general(
                cents[j][:, :width],
                row_ref[...],
                (((1,), (1,)), ((), ())),
                preferred_element_type=jnp.float32,
            )
            logits = (dots - half) * scale
            peak = jnp.max(logits, axis=0, keepdims=True)
            exp_values = jnp.exp(logits - peak)
            exps[j][:, start:stop] = exp_values
            stat_ref[base + j : base + j + 1, start:stop] = peak
            stat_ref[base + SIDE + j : base + SIDE + j + 1, start:stop] = jnp.sum(
                exp_values, axis=0, keepdims=True
            )
            start = stop


def norm_kernel(pos_ref, all_ref, own_ref, scale_ref, log_ref, sum_ref):
    me = pos_ref[0]
    allow_base = 2 * SIDE

    def allowed(r):
        return all_ref[r, 0 : SIDE * SIDE, :]

    def stat_rows(ref, index):
        start = SIDE * SIDE + index * allow_base
        return ref[start : start + SIDE, :], ref[start + SIDE : start + 2 * SIDE, :]

    logs = []
    for r in range(SIDE):
        allow = allowed(r)
        peaks, totals = [], []
        for q in range(SIDE):
            peak, total = stat_rows(all_ref.at[q], SHIFTS.index((r - q) % SIDE))
            peaks.append(peak)
            totals.append(total)
        peak = jnp.concatenate(peaks, axis=0)
        total = jnp.concatenate(totals, axis=0)
        top = jnp.max(jnp.where(allow > 0, peak, FLOOR), axis=0, keepdims=True)
        parts = jnp.where(allow > 0, total * jnp.exp(jnp.minimum(peak - top, 0.0)), 0.0)
        logs.append(top + jnp.log(jnp.sum(parts, axis=0, keepdims=True)))
    row_sum = logs[0] + logs[1] + logs[2] + logs[3]
    sum_ref[...] = jnp.broadcast_to(jnp.sum(row_sum, axis=1, keepdims=True), sum_ref.shape)
    for t in range(SIDE):
        place = lax.rem(me + SHIFTS[t], SIDE)
        log_t = jnp.zeros_like(logs[0])
        allow_t = jnp.zeros((SIDE, log_t.shape[1]), jnp.float32)
        for r in range(SIDE):
            here = place == r
            log_t = jnp.where(here, logs[r], log_t)
            for q in range(SIDE):
                allow_t = jnp.where(
                    jnp.logical_and(here, me == q), allowed(r)[q * SIDE : (q + 1) * SIDE, :], allow_t
                )
        peak, _ = stat_rows(own_ref, t)
        scale_ref[t * SIDE : (t + 1) * SIDE, :] = jnp.where(
            allow_t > 0, jnp.exp(jnp.minimum(peak - log_t, 0.0)), 0.0
        )
        if t == 0:
            log_ref[...] = log_t


def weighted(j, scale_ref, exps, rows):
    total, lanes = None, None
    for t in range(SIDE):
        weights = exps[t][...] * scale_ref[t * SIDE + j : t * SIDE + j + 1, :]
        for start in range(0, weights.shape[1], PAD):
            piece = weights[:, start : start + PAD]
            lanes = piece if lanes is None else lanes + piece
        rounded = weights.astype(jnp.bfloat16)
        start = 0
        for row_ref in rows[t]:
            stop = start + row_ref.shape[0]
            term = jnp.dot(
                rounded[:, start:stop], row_ref[...], preferred_element_type=jnp.float32
            )
            total = term if total is None else total + term
            start = stop
    return total, jnp.sum(lanes, axis=1, keepdims=True)


def sums_kernel(scale_ref, *refs):
    n_rows = SIDE + 1
    flat, row_refs = refs[: SIDE * SIDE], refs[SIDE * SIDE : SIDE * SIDE + n_rows]
    outs = refs[SIDE * SIDE + n_rows :]
    rows = [[row_refs[0]], [row_refs[1]], [row_refs[2]], [row_refs[3], row_refs[4]]]
    width = row_refs[0].shape[1]
    for j in range(SIDE - 1, -1, -1):
        exps = [flat[t * SIDE + j] for t in range(SIDE)]
        total, counts = weighted(j, scale_ref, exps, rows)
        if j == 0:
            outs[0][...] = total
            outs[SIDE][...] = jnp.broadcast_to(counts, outs[SIDE].shape)
        else:
            outs[j][:, :width] = total.astype(jnp.bfloat16)
            outs[j][:, width:] = tail_lanes(counts)


def final_kernel(total_ref, count_ref, a_ref, b_ref, c_ref, old_ref, out_ref):
    width = total_ref.shape[1]
    total = total_ref[...] + old_ref[...]
    counts = count_ref[:, 0:1] + 1.0
    for ref in (a_ref, b_ref, c_ref):
        total = total + ref[:, :width].astype(jnp.float32)
        counts = counts + read_tail(ref, width)
    out_ref[...] = total / counts


def call(kernel, outs, n_in, limit, flops=0, nbytes=0, smem=0):
    vmem = pl.BlockSpec(memory_space=pltpu.VMEM)
    scalar = pl.BlockSpec(memory_space=pltpu.SMEM)
    in_specs = [scalar] * smem + [vmem] * (n_in - smem)
    return pl.pallas_call(
        kernel,
        out_shape=outs,
        in_specs=in_specs,
        out_specs=jax.tree.map(lambda _: vmem, outs),
        cost_estimate=pl.CostEstimate(flops=flops, bytes_accessed=nbytes, transcendentals=0),
        compiler_params=pltpu.CompilerParams(vmem_limit_bytes=limit << 20),
    )


def bulk(value, pairs):
    return lax.ppermute(value, AXES, pairs)


def step(embeddings, centroids, candidates):
    planes = lax.axis_size("dp") // CORES
    core = lax.axis_index("dp") % CORES
    cent_index = lax.axis_index("cent")
    x, y = cent_index // SIDE, cent_index % SIDE
    row_pos = jnp.where(core == 0, x, y)
    cent_pos = jnp.where(core == 0, y, x)
    row_len, width = embeddings.shape
    f32, bf16 = jnp.float32, jnp.bfloat16
    shape = jax.ShapeDtypeStruct

    packed = call(pack_kernel, shape((BLK, width + PAD), bf16), 1, 8, nbytes=2 << 20)(centroids)
    cents = [packed] + [bulk(packed, cent_pairs(planes, SHIFTS[t])) for t in range(1, SIDE)]
    near = bulk(embeddings, row_pairs(planes, 1))
    back = bulk(embeddings, row_pairs(planes, SIDE - 1))
    half = row_len // 2
    far = [bulk(near[:half], row_pairs(planes, 1)), bulk(back[half:], row_pairs(planes, SIDE - 1))]
    rows = [[embeddings], [near], [back], far]

    pos = jnp.stack([row_pos, core, cent_pos]).astype(jnp.int32)
    exps, stats = [], []
    pair_flops = 2 * row_len * SIDE * BLK * width
    for t in range(SIDE):
        extra = stats if t == SIDE - 1 else []
        stat_rows = 2 * SIDE + sum(part.shape[0] for part in extra)
        scalars = (pos, candidates) if t == 0 else ()
        if t == 0:
            stat_rows += SIDE * SIDE
            kernel = functools.partial(first_score_kernel, 1.0 / width**0.5)
        else:
            kernel = functools.partial(
                score_kernel, 1.0 / width**0.5, len(rows[t]), len(extra)
            )
        *exp_values, stat = call(
            kernel,
            [shape((BLK, row_len), f32)] * SIDE + [shape((stat_rows, row_len), f32)],
            len(scalars) + len(rows[t]) + SIDE + len(extra),
            12,
            flops=pair_flops,
            nbytes=6 << 20,
            smem=len(scalars),
        )(*scalars, *rows[t], *cents, *extra)
        exps.append(exp_values)
        stats.append(stat)
    own_stats = stats[-1]
    all_stats = lax.all_gather(own_stats, AXES, axis_index_groups=row_lines(planes))
    n_cover = planes * CORES * SIDE
    scale, log_rows, line_sum = call(
        norm_kernel,
        [shape((SIDE * SIDE, row_len), f32), shape((1, row_len), f32), shape((n_cover, PAD), f32)],
        3,
        4,
        nbytes=1 << 20,
        smem=1,
    )(pos, all_stats, own_stats)

    total, *sent, counts = call(
        sums_kernel,
        [shape((BLK, width), f32)]
        + [shape((BLK, width + PAD), bf16)] * (SIDE - 1)
        + [shape((BLK, PAD), f32)],
        2 + SIDE * SIDE + SIDE,
        24,
        flops=SIDE * pair_flops,
        nbytes=16 << 20,
    )(scale, *[value for values in exps for value in values], *[part for parts in rows for part in parts])
    line_sum, total = lax.optimization_barrier((line_sum, total))
    cover_sums = lax.all_to_all(
        line_sum, AXES, 0, 0, tiled=True, axis_index_groups=line_covers(planes)
    )
    received = [bulk(sent[j - 1], cent_pairs(planes, -SHIFTS[j] % SIDE)) for j in (3, 1, 2)]
    tile = BLK // 2
    spec = lambda cols: pl.BlockSpec((tile, cols), lambda i: (i, 0))
    new_centroids = pl.pallas_call(
        final_kernel,
        name="final",
        grid=(BLK // tile,),
        out_shape=shape((BLK, width), f32),
        in_specs=[spec(width), spec(PAD)] + [spec(width + PAD)] * 3 + [spec(width)],
        out_specs=spec(width),
        cost_estimate=pl.CostEstimate(flops=0, bytes_accessed=5 << 20, transcendentals=0),
        compiler_params=pltpu.CompilerParams(vmem_limit_bytes=8 << 20),
    )(total, counts, *received, centroids)
    n_rows = row_len * lax.axis_size("dp") * SIDE * SIDE
    new_centroids, cover_sums = lax.optimization_barrier((new_centroids, cover_sums))
    objective = jnp.sum(cover_sums[:, 0]) / n_rows
    return new_centroids, log_rows.reshape(row_len), objective


def solution(mesh):
    in_specs = (P(AXES, None), P(AXES, None), P(AXES, None))
    out_specs = (P(AXES, None), P(AXES), P())
    return jax.shard_map(step, mesh=mesh, in_specs=in_specs, out_specs=out_specs, check_vma=False)
```

```python
import functools

import jax
import jax.numpy as jnp
from jax import lax
from jax.experimental import pallas as pl
from jax.experimental.pallas import tpu as pltpu
from jax.sharding import PartitionSpec as P


BLK = 256
SIDE = 4
CORES = 2
PAD = 128
AXES = ("dp", "cent")
SHIFTS = (0, 1, 3, 2)
FLOOR = -1e30
NEAR = ((0, None), (1, 1), (2, 0), (3, 0), (3, 1))
FAR = ((1, 0), (2, 1))


def device_at(plane, core, x, y):
    return (plane * CORES + core) * SIDE * SIDE + x * SIDE + y


def line_device(plane, core, row_pos, cent_pos):
    if core == 0:
        return device_at(plane, core, row_pos, cent_pos)
    return device_at(plane, core, cent_pos, row_pos)


def row_pairs(planes, shift):
    return [
        (line_device(z, c, r ^ shift, k), line_device(z, c, r, k))
        for z in range(planes)
        for c in range(CORES)
        for r in range(SIDE)
        for k in range(SIDE)
    ]


def cent_pairs(planes, shift):
    return [
        (line_device(z, c, r, k ^ shift), line_device(z, c, r, k))
        for z in range(planes)
        for c in range(CORES)
        for r in range(SIDE)
        for k in range(SIDE)
    ]


def row_lines(planes):
    return [
        [line_device(z, c, r, k) for r in range(SIDE)]
        for z in range(planes)
        for c in range(CORES)
        for k in range(SIDE)
    ]


def line_covers(planes):
    return [
        [line_device(z, c, r, k) for c in range(CORES) for z in range(planes) for k in range(SIDE)]
        for r in range(SIDE)
    ]


def split3(value):
    high = value.astype(jnp.bfloat16)
    rest = value - high.astype(jnp.float32)
    middle = rest.astype(jnp.bfloat16)
    low = (rest - middle.astype(jnp.float32)).astype(jnp.bfloat16)
    return high, middle, low


def tail_lanes(value):
    high, middle, low = (part.astype(jnp.float32) for part in split3(value))
    lane = lax.broadcasted_iota(jnp.int32, (value.shape[0], PAD), 1)
    tail = jnp.where(lane == 0, high, jnp.where(lane == 1, middle, jnp.where(lane == 2, low, 0.0)))
    return tail.astype(jnp.bfloat16)


def read_tail(ref, width):
    tail = ref[:, width:].astype(jnp.float32)
    return tail[:, 0:1] + tail[:, 1:2] + tail[:, 2:3]


def pack_kernel(cent_ref, out_ref):
    width = cent_ref.shape[1]
    values = cent_ref[...]
    out_ref[:, :width] = values.astype(jnp.bfloat16)
    out_ref[:, width:] = tail_lanes(0.5 * jnp.sum(values * values, axis=1, keepdims=True))


def split_kernel(row_ref, first_ref, second_ref, sems):
    half = first_ref.shape[0]
    copies = [
        pltpu.make_async_copy(row_ref.at[pl.ds(i * half, half), :], out_ref, sems.at[i])
        for i, out_ref in enumerate((first_ref, second_ref))
    ]
    for copy in copies:
        copy.start()
    for copy in copies:
        copy.wait()


def allow_rows(pos_ref, list_ref, stat_ref):
    core, cent_pos = pos_ref[1], pos_ref[2]
    row_len = stat_ref.shape[1]
    second = lax.broadcasted_iota(jnp.int32, (1, row_len), 1) >= row_len // 2
    for q in range(SIDE):
        for j in range(SIDE):
            other = cent_pos ^ SHIFTS[j]
            block = jnp.where(core == 0, q * SIDE + other, other * SIDE + q)
            hits = []
            for b in range(list_ref.shape[0]):
                hit = list_ref[b, 0] == block
                for i in range(1, list_ref.shape[1]):
                    hit = jnp.logical_or(hit, list_ref[b, i] == block)
                hits.append(jnp.where(hit, 1.0, 0.0))
            stat_ref[q * SIDE + j : q * SIDE + j + 1, :] = jnp.where(second, hits[1], hits[0])


def near_score_kernel(scale, pos_ref, list_ref, *refs):
    allow_rows(pos_ref, list_ref, refs[-1])
    n = len(NEAR)
    rows, cents, exps = refs[:n], refs[n : n + SIDE], refs[n + SIDE : -1]
    score(scale, NEAR, rows, cents, exps, refs[-1])


def far_score_kernel(scale, *refs):
    n = len(FAR)
    rows, cents, before_ref = refs[:n], refs[n : n + SIDE], refs[n + SIDE]
    exps, stat_ref = refs[n + SIDE + 1 : -1], refs[-1]
    stat_ref[...] = before_ref[...]
    score(scale, FAR, rows, cents, exps, stat_ref)


def lanes_of(half, row_ref):
    start = row_ref.shape[0] if half == 1 else 0
    return slice(start, start + row_ref.shape[0])


def score(scale, pieces, rows, cents, exps, stat_ref):
    width = rows[0].shape[1]
    for j in range(SIDE):
        half_norm = read_tail(cents[j], width)
        for i, (t, half) in enumerate(pieces):
            line = SIDE * SIDE + 2 * SIDE * t + j
            lanes = lanes_of(half, rows[i])
            dots = lax.dot_general(
                cents[j][:, :width],
                rows[i][...],
                (((1,), (1,)), ((), ())),
                preferred_element_type=jnp.float32,
            )
            logits = (dots - half_norm) * scale
            peak = jnp.max(logits, axis=0, keepdims=True)
            exp_values = jnp.exp(logits - peak)
            exps[i * SIDE + j][...] = exp_values
            stat_ref[line : line + 1, lanes] = peak
            stat_ref[line + SIDE : line + SIDE + 1, lanes] = jnp.sum(
                exp_values, axis=0, keepdims=True
            )


def norm_kernel(pos_ref, all_ref, own_ref, scale_ref, log_ref, sum_ref):
    me = pos_ref[0]
    allow_base = 2 * SIDE

    def allowed(r):
        return all_ref[r, 0 : SIDE * SIDE, :]

    def stat_rows(ref, index):
        start = SIDE * SIDE + index * allow_base
        return ref[start : start + SIDE, :], ref[start + SIDE : start + 2 * SIDE, :]

    logs = []
    for r in range(SIDE):
        allow = allowed(r)
        peaks, totals = [], []
        for q in range(SIDE):
            peak, total = stat_rows(all_ref.at[q], SHIFTS.index(r ^ q))
            peaks.append(peak)
            totals.append(total)
        peak = jnp.concatenate(peaks, axis=0)
        total = jnp.concatenate(totals, axis=0)
        top = jnp.max(jnp.where(allow > 0, peak, FLOOR), axis=0, keepdims=True)
        parts = jnp.where(allow > 0, total * jnp.exp(jnp.minimum(peak - top, 0.0)), 0.0)
        logs.append(top + jnp.log(jnp.sum(parts, axis=0, keepdims=True)))
    row_sum = logs[0] + logs[1] + logs[2] + logs[3]
    sum_ref[...] = jnp.broadcast_to(jnp.sum(row_sum, axis=1, keepdims=True), sum_ref.shape)
    for t in range(SIDE):
        place = me ^ SHIFTS[t]
        log_t = jnp.zeros_like(logs[0])
        allow_t = jnp.zeros((SIDE, log_t.shape[1]), jnp.float32)
        for r in range(SIDE):
            here = place == r
            log_t = jnp.where(here, logs[r], log_t)
            for q in range(SIDE):
                allow_t = jnp.where(
                    jnp.logical_and(here, me == q), allowed(r)[q * SIDE : (q + 1) * SIDE, :], allow_t
                )
        peak, _ = stat_rows(own_ref, t)
        scale_ref[t * SIDE : (t + 1) * SIDE, :] = jnp.where(
            allow_t > 0, jnp.exp(jnp.minimum(peak - log_t, 0.0)), 0.0
        )
        if t == 0:
            log_ref[...] = log_t


def weighted(j, scale_ref, exps, rows):
    total, lanes = None, None
    for i, (t, half) in enumerate(NEAR + FAR):
        line = t * SIDE + j
        weights = exps[i * SIDE + j][...] * scale_ref[line : line + 1, lanes_of(half, rows[i])]
        for start in range(0, weights.shape[1], PAD):
            piece = weights[:, start : start + PAD]
            lanes = piece if lanes is None else lanes + piece
        term = jnp.dot(
            weights.astype(jnp.bfloat16), rows[i][...], preferred_element_type=jnp.float32
        )
        total = term if total is None else total + term
    return total, jnp.sum(lanes, axis=1, keepdims=True)


def sums_kernel(scale_ref, *refs):
    n_rows = len(NEAR) + len(FAR)
    exps, rows = refs[: n_rows * SIDE], refs[n_rows * SIDE : n_rows * (SIDE + 1)]
    outs = refs[n_rows * (SIDE + 1) :]
    width = rows[0].shape[1]
    for j in range(SIDE - 1, -1, -1):
        total, counts = weighted(j, scale_ref, exps, rows)
        if j == 0:
            outs[0][...] = total
            outs[SIDE][...] = jnp.broadcast_to(counts, outs[SIDE].shape)
        else:
            outs[j][:, :width] = total.astype(jnp.bfloat16)
            outs[j][:, width:] = tail_lanes(counts)


def final_kernel(total_ref, count_ref, a_ref, b_ref, c_ref, old_ref, out_ref):
    width = total_ref.shape[1]
    total = total_ref[...] + old_ref[...]
    counts = count_ref[:, 0:1] + 1.0
    for ref in (a_ref, b_ref, c_ref):
        total = total + ref[:, :width].astype(jnp.float32)
        counts = counts + read_tail(ref, width)
    out_ref[...] = total / counts


def call(kernel, outs, n_in, limit, flops=0, nbytes=0, smem=0):
    vmem = pl.BlockSpec(memory_space=pltpu.VMEM)
    scalar = pl.BlockSpec(memory_space=pltpu.SMEM)
    in_specs = [scalar] * smem + [vmem] * (n_in - smem)
    return pl.pallas_call(
        kernel,
        out_shape=outs,
        in_specs=in_specs,
        out_specs=jax.tree.map(lambda _: vmem, outs),
        cost_estimate=pl.CostEstimate(flops=flops, bytes_accessed=nbytes, transcendentals=0),
        compiler_params=pltpu.CompilerParams(vmem_limit_bytes=limit << 20),
    )


def bulk(value, pairs):
    return lax.ppermute(value, AXES, pairs)


def step(embeddings, centroids, candidates):
    planes = lax.axis_size("dp") // CORES
    core = lax.axis_index("dp") % CORES
    cent_index = lax.axis_index("cent")
    x, y = cent_index // SIDE, cent_index % SIDE
    row_pos = jnp.where(core == 0, x, y)
    cent_pos = jnp.where(core == 0, y, x)
    row_len, width = embeddings.shape
    f32, bf16 = jnp.float32, jnp.bfloat16
    shape = jax.ShapeDtypeStruct

    packed = call(pack_kernel, shape((BLK, width + PAD), bf16), 1, 8, nbytes=2 << 20)(centroids)
    cents = [packed] + [bulk(packed, cent_pairs(planes, SHIFTS[t])) for t in range(1, SIDE)]
    half = row_len // 2
    halves = pl.pallas_call(
        split_kernel,
        name="split",
        out_shape=[shape((half, width), bf16)] * 2,
        in_specs=[pl.BlockSpec(memory_space=pl.ANY)],
        out_specs=[pl.BlockSpec(memory_space=pltpu.VMEM)] * 2,
        scratch_shapes=[pltpu.SemaphoreType.DMA((2,))],
        cost_estimate=pl.CostEstimate(flops=0, bytes_accessed=2 << 20, transcendentals=0),
        compiler_params=pltpu.CompilerParams(vmem_limit_bytes=4 << 20),
    )(embeddings)
    piece = {(0, None): embeddings}
    for t in (1, 2):
        for h in (0, 1):
            piece[t, h] = bulk(halves[h], row_pairs(planes, SHIFTS[t]))
    piece[3, 1] = bulk(piece[1, 1], row_pairs(planes, SHIFTS[2]))
    piece[3, 0] = bulk(piece[2, 0], row_pairs(planes, SHIFTS[1]))
    near = [piece[key] for key in NEAR]
    far = [piece[key] for key in FAR]
    rows = near + far

    pos = jnp.stack([row_pos, core, cent_pos]).astype(jnp.int32)
    pair_flops = 2 * row_len * SIDE * BLK * width
    factor = 1.0 / width**0.5
    stat_shape = shape((SIDE * SIDE + 2 * SIDE * SIDE, row_len), f32)

    def exp_shapes(values):
        return [shape((BLK, value.shape[0]), f32) for value in values for _ in range(SIDE)]

    *near_exps, near_stats = call(
        functools.partial(near_score_kernel, factor),
        exp_shapes(near) + [stat_shape],
        2 + len(near) + SIDE,
        16,
        flops=3 * pair_flops,
        nbytes=14 << 20,
        smem=2,
    )(pos, candidates, *near, *cents)
    *far_exps, own_stats = call(
        functools.partial(far_score_kernel, factor),
        exp_shapes(far) + [stat_shape],
        len(far) + SIDE + 1,
        12,
        flops=pair_flops,
        nbytes=6 << 20,
    )(*far, *cents, near_stats)
    exps = near_exps + far_exps
    all_stats = lax.all_gather(own_stats, AXES, axis_index_groups=row_lines(planes))
    n_cover = planes * CORES * SIDE
    scale, log_rows, line_sum = call(
        norm_kernel,
        [shape((SIDE * SIDE, row_len), f32), shape((1, row_len), f32), shape((n_cover, PAD), f32)],
        3,
        4,
        nbytes=1 << 20,
        smem=1,
    )(row_pos.reshape(1).astype(jnp.int32), all_stats, own_stats)

    total, *sent, counts = call(
        sums_kernel,
        [shape((BLK, width), f32)]
        + [shape((BLK, width + PAD), bf16)] * (SIDE - 1)
        + [shape((BLK, PAD), f32)],
        1 + len(exps) + len(rows),
        24,
        flops=SIDE * pair_flops,
        nbytes=16 << 20,
    )(scale, *exps, *rows)
    line_sum, total = lax.optimization_barrier((line_sum, total))
    cover_sums = lax.all_to_all(
        line_sum, AXES, 0, 0, tiled=True, axis_index_groups=line_covers(planes)
    )
    received = [bulk(sent[j - 1], cent_pairs(planes, SHIFTS[j])) for j in (3, 2, 1)]
    tile = BLK // 2
    spec = lambda cols: pl.BlockSpec((tile, cols), lambda i: (i, 0))
    new_centroids = pl.pallas_call(
        final_kernel,
        name="final",
        grid=(BLK // tile,),
        out_shape=shape((BLK, width), f32),
        in_specs=[spec(width), spec(PAD)] + [spec(width + PAD)] * 3 + [spec(width)],
        out_specs=spec(width),
        cost_estimate=pl.CostEstimate(flops=0, bytes_accessed=5 << 20, transcendentals=0),
        compiler_params=pltpu.CompilerParams(vmem_limit_bytes=8 << 20),
    )(total, counts, *received, centroids)
    n_rows = row_len * lax.axis_size("dp") * SIDE * SIDE
    new_centroids, cover_sums = lax.optimization_barrier((new_centroids, cover_sums))
    objective = jnp.sum(cover_sums[:, 0]) / n_rows
    return new_centroids, log_rows.reshape(row_len), objective


def solution(mesh):
    in_specs = (P(AXES, None), P(AXES, None), P(AXES, None))
    out_specs = (P(AXES, None), P(AXES), P())
    return jax.shard_map(step, mesh=mesh, in_specs=in_specs, out_specs=out_specs, check_vma=False)
```

```python
import functools

import jax
import jax.numpy as jnp
from jax import lax
from jax.experimental import pallas as pl
from jax.experimental.pallas import tpu as pltpu
from jax.sharding import PartitionSpec as P


BLK = 256
SIDE = 4
CORES = 2
PAD = 128
AXES = ("dp", "cent")
SHIFTS = (0, 1, 3, 2)
FLOOR = -1e30
NEAR = ((0, None), (1, 1), (2, 0), (3, 0), (3, 1))
FAR = ((1, 0), (2, 1))


def device_at(plane, core, x, y):
    return (plane * CORES + core) * SIDE * SIDE + x * SIDE + y


def line_device(plane, core, row_pos, cent_pos):
    if core == 0:
        return device_at(plane, core, row_pos, cent_pos)
    return device_at(plane, core, cent_pos, row_pos)


def row_pairs(planes, shift):
    return [
        (line_device(z, c, r ^ shift, k), line_device(z, c, r, k))
        for z in range(planes)
        for c in range(CORES)
        for r in range(SIDE)
        for k in range(SIDE)
    ]


def cent_pairs(planes, shift):
    return [
        (line_device(z, c, r, k ^ shift), line_device(z, c, r, k))
        for z in range(planes)
        for c in range(CORES)
        for r in range(SIDE)
        for k in range(SIDE)
    ]


def cent_lines(planes):
    return [
        [line_device(z, c, r, k) for k in range(SIDE)]
        for z in range(planes)
        for c in range(CORES)
        for r in range(SIDE)
    ]


def row_lines(planes):
    return [
        [line_device(z, c, r, k) for r in range(SIDE)]
        for z in range(planes)
        for c in range(CORES)
        for k in range(SIDE)
    ]


def line_covers(planes):
    return [
        [line_device(z, c, r, k) for c in range(CORES) for z in range(planes) for k in range(SIDE)]
        for r in range(SIDE)
    ]


def split3(value):
    high = value.astype(jnp.bfloat16)
    rest = value - high.astype(jnp.float32)
    middle = rest.astype(jnp.bfloat16)
    low = (rest - middle.astype(jnp.float32)).astype(jnp.bfloat16)
    return high, middle, low


def tail_lanes(value):
    high, middle, low = (part.astype(jnp.float32) for part in split3(value))
    lane = lax.broadcasted_iota(jnp.int32, (value.shape[0], PAD), 1)
    tail = jnp.where(lane == 0, high, jnp.where(lane == 1, middle, jnp.where(lane == 2, low, 0.0)))
    return tail.astype(jnp.bfloat16)


def read_tail(ref, width):
    tail = ref[:, width:].astype(jnp.float32)
    return tail[:, 0:1] + tail[:, 1:2] + tail[:, 2:3]


def pack_kernel(cent_ref, out_ref):
    width = cent_ref.shape[1]
    values = cent_ref[...]
    rounded = values.astype(jnp.bfloat16)
    tail = tail_lanes(0.5 * jnp.sum(values * values, axis=1, keepdims=True))
    for j in range(SIDE):
        out_ref[j, :, :width] = rounded
        out_ref[j, :, width:] = tail


def split_kernel(row_ref, first_ref, second_ref, sems):
    half = first_ref.shape[0]
    copies = [
        pltpu.make_async_copy(row_ref.at[pl.ds(i * half, half), :], out_ref, sems.at[i])
        for i, out_ref in enumerate((first_ref, second_ref))
    ]
    for copy in copies:
        copy.start()
    for copy in copies:
        copy.wait()


def allow_rows(pos_ref, list_ref, stat_ref):
    core = pos_ref[1]
    row_len = stat_ref.shape[1]
    second = lax.broadcasted_iota(jnp.int32, (1, row_len), 1) >= row_len // 2
    for q in range(SIDE):
        for j in range(SIDE):
            block = jnp.where(core == 0, q * SIDE + j, j * SIDE + q)
            hits = []
            for b in range(list_ref.shape[0]):
                hit = list_ref[b, 0] == block
                for i in range(1, list_ref.shape[1]):
                    hit = jnp.logical_or(hit, list_ref[b, i] == block)
                hits.append(jnp.where(hit, 1.0, 0.0))
            stat_ref[q * SIDE + j : q * SIDE + j + 1, :] = jnp.where(second, hits[1], hits[0])


def near_score_kernel(scale, pos_ref, list_ref, *refs):
    allow_rows(pos_ref, list_ref, refs[-1])
    n = len(NEAR)
    rows, cents, exps = refs[:n], refs[n], refs[n + 1 : -1]
    score(scale, NEAR, rows, cents, exps, refs[-1])


def far_score_kernel(scale, *refs):
    n = len(FAR)
    rows, cents, before_ref = refs[:n], refs[n], refs[n + 1]
    exps, stat_ref = refs[n + 2 : -1], refs[-1]
    stat_ref[...] = before_ref[...]
    score(scale, FAR, rows, cents, exps, stat_ref)


def lanes_of(half, row_ref):
    start = row_ref.shape[0] if half == 1 else 0
    return slice(start, start + row_ref.shape[0])


def score(scale, pieces, rows, cents, exps, stat_ref):
    width = rows[0].shape[1]
    for j in range(SIDE):
        half_norm = read_tail(cents.at[j], width)
        for i, (t, half) in enumerate(pieces):
            line = SIDE * SIDE + 2 * SIDE * t + j
            lanes = lanes_of(half, rows[i])
            dots = lax.dot_general(
                cents[j, :, :width],
                rows[i][...],
                (((1,), (1,)), ((), ())),
                preferred_element_type=jnp.float32,
            )
            logits = (dots - half_norm) * scale
            peak = jnp.max(logits, axis=0, keepdims=True)
            exp_values = jnp.exp(logits - peak)
            exps[i][j] = exp_values
            stat_ref[line : line + 1, lanes] = peak
            stat_ref[line + SIDE : line + SIDE + 1, lanes] = jnp.sum(
                exp_values, axis=0, keepdims=True
            )


def norm_kernel(pos_ref, all_ref, own_ref, scale_ref, log_ref, sum_ref):
    me = pos_ref[0]
    allow_base = 2 * SIDE

    def allowed(r):
        return all_ref[r, 0 : SIDE * SIDE, :]

    def stat_rows(ref, index):
        start = SIDE * SIDE + index * allow_base
        return ref[start : start + SIDE, :], ref[start + SIDE : start + 2 * SIDE, :]

    logs = []
    for r in range(SIDE):
        allow = allowed(r)
        peaks, totals = [], []
        for q in range(SIDE):
            peak, total = stat_rows(all_ref.at[q], SHIFTS.index(r ^ q))
            peaks.append(peak)
            totals.append(total)
        peak = jnp.concatenate(peaks, axis=0)
        total = jnp.concatenate(totals, axis=0)
        top = jnp.max(jnp.where(allow > 0, peak, FLOOR), axis=0, keepdims=True)
        parts = jnp.where(allow > 0, total * jnp.exp(jnp.minimum(peak - top, 0.0)), 0.0)
        logs.append(top + jnp.log(jnp.sum(parts, axis=0, keepdims=True)))
    row_sum = logs[0] + logs[1] + logs[2] + logs[3]
    sum_ref[...] = jnp.broadcast_to(jnp.sum(row_sum, axis=1, keepdims=True), sum_ref.shape)
    for t in range(SIDE):
        place = me ^ SHIFTS[t]
        log_t = jnp.zeros_like(logs[0])
        allow_t = jnp.zeros((SIDE, log_t.shape[1]), jnp.float32)
        for r in range(SIDE):
            here = place == r
            log_t = jnp.where(here, logs[r], log_t)
            for q in range(SIDE):
                allow_t = jnp.where(
                    jnp.logical_and(here, me == q), allowed(r)[q * SIDE : (q + 1) * SIDE, :], allow_t
                )
        peak, _ = stat_rows(own_ref, t)
        scale_ref[t * SIDE : (t + 1) * SIDE, :] = jnp.where(
            allow_t > 0, jnp.exp(jnp.minimum(peak - log_t, 0.0)), 0.0
        )
        if t == 0:
            log_ref[...] = log_t


def weighted(j, scale_ref, exps, rows):
    total, lanes = None, None
    for i, (t, half) in enumerate(NEAR + FAR):
        factor = scale_ref[pl.ds(t * SIDE + j, 1), lanes_of(half, rows[i])]
        weights = exps[i][j] * factor
        for start in range(0, weights.shape[1], PAD):
            piece = weights[:, start : start + PAD]
            lanes = piece if lanes is None else lanes + piece
        term = jnp.dot(
            weights.astype(jnp.bfloat16), rows[i][...], preferred_element_type=jnp.float32
        )
        total = term if total is None else total + term
    return total, jnp.sum(lanes, axis=1, keepdims=True)


def sums_kernel(pos_ref, scale_ref, *refs):
    n_rows = len(NEAR) + len(FAR)
    exps, rows, outs = refs[:n_rows], refs[n_rows : 2 * n_rows], refs[2 * n_rows :]
    width = rows[0].shape[1]
    for i in range(SIDE - 1, -1, -1):
        total, counts = weighted(pos_ref[0] ^ SHIFTS[i], scale_ref, exps, rows)
        if i == 0:
            outs[0][...] = total
            outs[SIDE][...] = jnp.broadcast_to(counts, outs[SIDE].shape)
        else:
            outs[i][:, :width] = total.astype(jnp.bfloat16)
            outs[i][:, width:] = tail_lanes(counts)


def final_kernel(total_ref, count_ref, a_ref, b_ref, c_ref, old_ref, out_ref):
    width = total_ref.shape[1]
    total = total_ref[...] + old_ref[...]
    counts = count_ref[:, 0:1] + 1.0
    for ref in (a_ref, b_ref, c_ref):
        total = total + ref[:, :width].astype(jnp.float32)
        counts = counts + read_tail(ref, width)
    out_ref[...] = total / counts


def call(kernel, outs, n_in, limit, flops=0, nbytes=0, smem=0):
    vmem = pl.BlockSpec(memory_space=pltpu.VMEM)
    scalar = pl.BlockSpec(memory_space=pltpu.SMEM)
    in_specs = [scalar] * smem + [vmem] * (n_in - smem)
    return pl.pallas_call(
        kernel,
        out_shape=outs,
        in_specs=in_specs,
        out_specs=jax.tree.map(lambda _: vmem, outs),
        cost_estimate=pl.CostEstimate(flops=flops, bytes_accessed=nbytes, transcendentals=0),
        compiler_params=pltpu.CompilerParams(vmem_limit_bytes=limit << 20),
    )


def bulk(value, pairs):
    return lax.ppermute(value, AXES, pairs)


def line_swap(value, groups):
    return lax.all_to_all(value, AXES, 0, 0, axis_index_groups=groups, tiled=True)


def step(embeddings, centroids, candidates):
    planes = lax.axis_size("dp") // CORES
    core = lax.axis_index("dp") % CORES
    cent_index = lax.axis_index("cent")
    x, y = cent_index // SIDE, cent_index % SIDE
    row_pos = jnp.where(core == 0, x, y)
    cent_pos = jnp.where(core == 0, y, x)
    row_len, width = embeddings.shape
    f32, bf16 = jnp.float32, jnp.bfloat16
    shape = jax.ShapeDtypeStruct

    block_shape = shape((SIDE, BLK, width + PAD), bf16)
    packed = call(pack_kernel, block_shape, 1, 8, nbytes=4 << 20)(centroids)
    cents = line_swap(packed, cent_lines(planes))
    half = row_len // 2
    halves = pl.pallas_call(
        split_kernel,
        name="split",
        out_shape=[shape((half, width), bf16)] * 2,
        in_specs=[pl.BlockSpec(memory_space=pl.ANY)],
        out_specs=[pl.BlockSpec(memory_space=pltpu.VMEM)] * 2,
        scratch_shapes=[pltpu.SemaphoreType.DMA((2,))],
        cost_estimate=pl.CostEstimate(flops=0, bytes_accessed=2 << 20, transcendentals=0),
        compiler_params=pltpu.CompilerParams(vmem_limit_bytes=4 << 20),
    )(embeddings)
    piece = {(0, None): embeddings}
    for t in (1, 2):
        for h in (0, 1):
            piece[t, h] = bulk(halves[h], row_pairs(planes, SHIFTS[t]))
    piece[3, 1] = bulk(piece[1, 1], row_pairs(planes, SHIFTS[2]))
    piece[3, 0] = bulk(piece[2, 0], row_pairs(planes, SHIFTS[1]))
    near = [piece[key] for key in NEAR]
    far = [piece[key] for key in FAR]
    rows = near + far

    pos = jnp.stack([row_pos, core, cent_pos]).astype(jnp.int32)
    pair_flops = 2 * row_len * SIDE * BLK * width
    factor = 1.0 / width**0.5
    stat_shape = shape((SIDE * SIDE + 2 * SIDE * SIDE, row_len), f32)

    def exp_shapes(values):
        return [shape((SIDE, BLK, value.shape[0]), f32) for value in values]

    *near_exps, near_stats = call(
        functools.partial(near_score_kernel, factor),
        exp_shapes(near) + [stat_shape],
        2 + len(near) + 1,
        16,
        flops=3 * pair_flops,
        nbytes=14 << 20,
        smem=2,
    )(pos, candidates, *near, cents)
    *far_exps, own_stats = call(
        functools.partial(far_score_kernel, factor),
        exp_shapes(far) + [stat_shape],
        len(far) + 2,
        12,
        flops=pair_flops,
        nbytes=6 << 20,
    )(*far, cents, near_stats)
    exps = near_exps + far_exps
    all_stats = lax.all_gather(own_stats, AXES, axis_index_groups=row_lines(planes))
    n_cover = planes * CORES * SIDE
    scale, log_rows, line_sum = call(
        norm_kernel,
        [shape((SIDE * SIDE, row_len), f32), shape((1, row_len), f32), shape((n_cover, PAD), f32)],
        3,
        4,
        nbytes=1 << 20,
        smem=1,
    )(row_pos.reshape(1).astype(jnp.int32), all_stats, own_stats)

    total, *sent, counts = call(
        sums_kernel,
        [shape((BLK, width), f32)]
        + [shape((BLK, width + PAD), bf16)] * (SIDE - 1)
        + [shape((BLK, PAD), f32)],
        2 + len(exps) + len(rows),
        24,
        flops=SIDE * pair_flops,
        nbytes=16 << 20,
        smem=1,
    )(cent_pos.reshape(1).astype(jnp.int32), scale, *exps, *rows)
    line_sum, total = lax.optimization_barrier((line_sum, total))
    cover_sums = lax.all_to_all(
        line_sum, AXES, 0, 0, tiled=True, axis_index_groups=line_covers(planes)
    )
    received = [bulk(sent[j - 1], cent_pairs(planes, SHIFTS[j])) for j in (3, 2, 1)]
    tile = BLK // 2
    spec = lambda cols: pl.BlockSpec((tile, cols), lambda i: (i, 0))
    new_centroids = pl.pallas_call(
        final_kernel,
        name="final",
        grid=(BLK // tile,),
        out_shape=shape((BLK, width), f32),
        in_specs=[spec(width), spec(PAD)] + [spec(width + PAD)] * 3 + [spec(width)],
        out_specs=spec(width),
        cost_estimate=pl.CostEstimate(flops=0, bytes_accessed=5 << 20, transcendentals=0),
        compiler_params=pltpu.CompilerParams(vmem_limit_bytes=8 << 20),
    )(total, counts, *received, centroids)
    n_rows = row_len * lax.axis_size("dp") * SIDE * SIDE
    new_centroids, cover_sums = lax.optimization_barrier((new_centroids, cover_sums))
    objective = jnp.sum(cover_sums[:, 0]) / n_rows
    return new_centroids, log_rows.reshape(row_len), objective


def solution(mesh):
    in_specs = (P(AXES, None), P(AXES, None), P(AXES, None))
    out_specs = (P(AXES, None), P(AXES), P())
    return jax.shard_map(step, mesh=mesh, in_specs=in_specs, out_specs=out_specs, check_vma=False)
```

```python
import functools

import jax
import jax.numpy as jnp
from jax import lax
from jax.experimental import pallas as pl
from jax.experimental.pallas import tpu as pltpu
from jax.sharding import PartitionSpec as P


BLK = 256
SIDE = 4
CORES = 2
PAD = 128
AXES = ("dp", "cent")
SHIFTS = (0, 1, 3, 2)
FLOOR = -1e30
NEAR = ((0, None), (1, 1), (2, 0), (3, 0), (3, 1))
FAR = ((1, 0), (2, 1))


def device_at(plane, core, x, y):
    return (plane * CORES + core) * SIDE * SIDE + x * SIDE + y


def line_device(plane, core, row_pos, cent_pos):
    if core == 0:
        return device_at(plane, core, row_pos, cent_pos)
    return device_at(plane, core, cent_pos, row_pos)


def row_pairs(planes, shift):
    return [
        (line_device(z, c, r ^ shift, k), line_device(z, c, r, k))
        for z in range(planes)
        for c in range(CORES)
        for r in range(SIDE)
        for k in range(SIDE)
    ]


def cent_pairs(planes, shift):
    return [
        (line_device(z, c, r, k ^ shift), line_device(z, c, r, k))
        for z in range(planes)
        for c in range(CORES)
        for r in range(SIDE)
        for k in range(SIDE)
    ]


def row_lines(planes):
    return [
        [line_device(z, c, r, k) for r in range(SIDE)]
        for z in range(planes)
        for c in range(CORES)
        for k in range(SIDE)
    ]


def line_covers(planes):
    return [
        [line_device(z, c, r, k) for c in range(CORES) for z in range(planes) for k in range(SIDE)]
        for r in range(SIDE)
    ]


def split3(value):
    high = value.astype(jnp.bfloat16)
    rest = value - high.astype(jnp.float32)
    middle = rest.astype(jnp.bfloat16)
    low = (rest - middle.astype(jnp.float32)).astype(jnp.bfloat16)
    return high, middle, low


def tail_lanes(value):
    high, middle, low = (part.astype(jnp.float32) for part in split3(value))
    lane = lax.broadcasted_iota(jnp.int32, (value.shape[0], PAD), 1)
    tail = jnp.where(lane == 0, high, jnp.where(lane == 1, middle, jnp.where(lane == 2, low, 0.0)))
    return tail.astype(jnp.bfloat16)


def read_tail(ref, width):
    tail = ref[:, width:].astype(jnp.float32)
    return tail[:, 0:1] + tail[:, 1:2] + tail[:, 2:3]


def pack_kernel(cent_ref, out_ref):
    width = cent_ref.shape[1]
    values = cent_ref[...]
    out_ref[:, :width] = values.astype(jnp.bfloat16)
    out_ref[:, width:] = tail_lanes(0.5 * jnp.sum(values * values, axis=1, keepdims=True))


def split_kernel(row_ref, first_ref, second_ref, sems):
    half = first_ref.shape[0]
    copies = [
        pltpu.make_async_copy(row_ref.at[pl.ds(i * half, half), :], out_ref, sems.at[i])
        for i, out_ref in enumerate((first_ref, second_ref))
    ]
    for copy in copies:
        copy.start()
    for copy in copies:
        copy.wait()


def allow_rows(pos_ref, list_ref, stat_ref):
    core, cent_pos = pos_ref[1], pos_ref[2]
    row_len = stat_ref.shape[1]
    second = lax.broadcasted_iota(jnp.int32, (1, row_len), 1) >= row_len // 2
    for q in range(SIDE):
        for j in range(SIDE):
            other = cent_pos ^ SHIFTS[j]
            block = jnp.where(core == 0, q * SIDE + other, other * SIDE + q)
            hits = []
            for b in range(list_ref.shape[0]):
                hit = list_ref[b, 0] == block
                for i in range(1, list_ref.shape[1]):
                    hit = jnp.logical_or(hit, list_ref[b, i] == block)
                hits.append(jnp.where(hit, 1.0, 0.0))
            stat_ref[q * SIDE + j : q * SIDE + j + 1, :] = jnp.where(second, hits[1], hits[0])


def near_score_kernel(scale, pos_ref, list_ref, *refs):
    allow_rows(pos_ref, list_ref, refs[-1])
    n = len(NEAR)
    rows, cents, exps = refs[:n], refs[n : n + SIDE], refs[n + SIDE : -1]
    score(scale, NEAR, rows, cents, exps, refs[-1])


def far_score_kernel(scale, *refs):
    n = len(FAR)
    rows, cents, before_ref = refs[:n], refs[n : n + SIDE], refs[n + SIDE]
    exps, stat_ref = refs[n + SIDE + 1 : -1], refs[-1]
    stat_ref[...] = before_ref[...]
    score(scale, FAR, rows, cents, exps, stat_ref)


def lanes_of(half, row_ref):
    start = row_ref.shape[0] if half == 1 else 0
    return slice(start, start + row_ref.shape[0])


def score(scale, pieces, rows, cents, exps, stat_ref):
    width = rows[0].shape[1]
    for j in range(SIDE):
        half_norm = read_tail(cents[j], width)
        for i, (t, half) in enumerate(pieces):
            line = SIDE * SIDE + 2 * SIDE * t + j
            lanes = lanes_of(half, rows[i])
            dots = lax.dot_general(
                cents[j][:, :width],
                rows[i][...],
                (((1,), (1,)), ((), ())),
                preferred_element_type=jnp.float32,
            )
            logits = (dots - half_norm) * scale
            peak = jnp.max(logits, axis=0, keepdims=True)
            exp_values = jnp.exp(logits - peak)
            exps[i * SIDE + j][...] = exp_values
            stat_ref[line : line + 1, lanes] = peak
            stat_ref[line + SIDE : line + SIDE + 1, lanes] = jnp.sum(
                exp_values, axis=0, keepdims=True
            )


def norm_factors(pos_ref, all_ref, own_ref, scale_ref, log_ref, sum_ref):
    me = pos_ref[0]
    allow_base = 2 * SIDE

    def allowed(r):
        return all_ref[r, 0 : SIDE * SIDE, :]

    def stat_rows(ref, index):
        start = SIDE * SIDE + index * allow_base
        return ref[start : start + SIDE, :], ref[start + SIDE : start + 2 * SIDE, :]

    logs = []
    for r in range(SIDE):
        allow = allowed(r)
        peaks, totals = [], []
        for q in range(SIDE):
            peak, total = stat_rows(all_ref.at[q], SHIFTS.index(r ^ q))
            peaks.append(peak)
            totals.append(total)
        peak = jnp.concatenate(peaks, axis=0)
        total = jnp.concatenate(totals, axis=0)
        top = jnp.max(jnp.where(allow > 0, peak, FLOOR), axis=0, keepdims=True)
        parts = jnp.where(allow > 0, total * jnp.exp(jnp.minimum(peak - top, 0.0)), 0.0)
        logs.append(top + jnp.log(jnp.sum(parts, axis=0, keepdims=True)))
    row_sum = logs[0] + logs[1] + logs[2] + logs[3]
    sum_ref[...] = jnp.broadcast_to(jnp.sum(row_sum, axis=1, keepdims=True), sum_ref.shape)
    for t in range(SIDE):
        place = me ^ SHIFTS[t]
        log_t = jnp.zeros_like(logs[0])
        allow_t = jnp.zeros((SIDE, log_t.shape[1]), jnp.float32)
        for r in range(SIDE):
            here = place == r
            log_t = jnp.where(here, logs[r], log_t)
            for q in range(SIDE):
                allow_t = jnp.where(
                    jnp.logical_and(here, me == q), allowed(r)[q * SIDE : (q + 1) * SIDE, :], allow_t
                )
        peak, _ = stat_rows(own_ref, t)
        scale_ref[t * SIDE : (t + 1) * SIDE, :] = jnp.where(
            allow_t > 0, jnp.exp(jnp.minimum(peak - log_t, 0.0)), 0.0
        )
        if t == 0:
            log_ref[...] = log_t


def weighted(j, scale_ref, exps, rows):
    total, lanes = None, None
    for i, (t, half) in enumerate(NEAR + FAR):
        line = t * SIDE + j
        weights = exps[i * SIDE + j][...] * scale_ref[line : line + 1, lanes_of(half, rows[i])]
        for start in range(0, weights.shape[1], PAD):
            piece = weights[:, start : start + PAD]
            lanes = piece if lanes is None else lanes + piece
        term = jnp.dot(
            weights.astype(jnp.bfloat16), rows[i][...], preferred_element_type=jnp.float32
        )
        total = term if total is None else total + term
    return total, jnp.sum(lanes, axis=1, keepdims=True)


def sums_kernel(pos_ref, all_ref, own_ref, *refs):
    n_rows = len(NEAR) + len(FAR)
    exps, rows = refs[: n_rows * SIDE], refs[n_rows * SIDE : n_rows * (SIDE + 1)]
    *outs, log_ref, sum_ref, scale_ref = refs[n_rows * (SIDE + 1) :]
    norm_factors(pos_ref, all_ref, own_ref, scale_ref, log_ref, sum_ref)
    width = rows[0].shape[1]
    for j in range(SIDE - 1, -1, -1):
        total, counts = weighted(j, scale_ref, exps, rows)
        if j == 0:
            outs[0][...] = total
            outs[SIDE][...] = jnp.broadcast_to(counts, outs[SIDE].shape)
        else:
            outs[j][:, :width] = total.astype(jnp.bfloat16)
            outs[j][:, width:] = tail_lanes(counts)


def final_kernel(total_ref, count_ref, a_ref, b_ref, c_ref, old_ref, out_ref):
    width = total_ref.shape[1]
    total = total_ref[...] + old_ref[...]
    counts = count_ref[:, 0:1] + 1.0
    for ref in (a_ref, b_ref, c_ref):
        total = total + ref[:, :width].astype(jnp.float32)
        counts = counts + read_tail(ref, width)
    out_ref[...] = total / counts


def call(kernel, outs, n_in, limit, flops=0, nbytes=0, smem=0, scratch=()):
    vmem = pl.BlockSpec(memory_space=pltpu.VMEM)
    scalar = pl.BlockSpec(memory_space=pltpu.SMEM)
    in_specs = [scalar] * smem + [vmem] * (n_in - smem)
    return pl.pallas_call(
        kernel,
        out_shape=outs,
        in_specs=in_specs,
        out_specs=jax.tree.map(lambda _: vmem, outs),
        scratch_shapes=scratch,
        cost_estimate=pl.CostEstimate(flops=flops, bytes_accessed=nbytes, transcendentals=0),
        compiler_params=pltpu.CompilerParams(vmem_limit_bytes=limit << 20),
    )


def bulk(value, pairs):
    return lax.ppermute(value, AXES, pairs)


def step(embeddings, centroids, candidates):
    planes = lax.axis_size("dp") // CORES
    core = lax.axis_index("dp") % CORES
    cent_index = lax.axis_index("cent")
    x, y = cent_index // SIDE, cent_index % SIDE
    row_pos = jnp.where(core == 0, x, y)
    cent_pos = jnp.where(core == 0, y, x)
    row_len, width = embeddings.shape
    f32, bf16 = jnp.float32, jnp.bfloat16
    shape = jax.ShapeDtypeStruct

    packed = call(pack_kernel, shape((BLK, width + PAD), bf16), 1, 8, nbytes=2 << 20)(centroids)
    cents = [packed] + [bulk(packed, cent_pairs(planes, SHIFTS[t])) for t in range(1, SIDE)]
    half = row_len // 2
    halves = pl.pallas_call(
        split_kernel,
        name="split",
        out_shape=[shape((half, width), bf16)] * 2,
        in_specs=[pl.BlockSpec(memory_space=pltpu.HBM)],
        out_specs=[pl.BlockSpec(memory_space=pltpu.VMEM)] * 2,
        scratch_shapes=[pltpu.SemaphoreType.DMA((2,))],
        cost_estimate=pl.CostEstimate(flops=0, bytes_accessed=2 << 20, transcendentals=0),
        compiler_params=pltpu.CompilerParams(vmem_limit_bytes=4 << 20),
    )(embeddings)
    piece = {(0, None): embeddings}
    for t in (1, 2):
        for h in (0, 1):
            piece[t, h] = bulk(halves[h], row_pairs(planes, SHIFTS[t]))
    piece[3, 1] = bulk(piece[1, 1], row_pairs(planes, SHIFTS[2]))
    piece[3, 0] = bulk(piece[2, 0], row_pairs(planes, SHIFTS[1]))
    near = [piece[key] for key in NEAR]
    far = [piece[key] for key in FAR]
    rows = near + far

    pos = jnp.stack([row_pos, core, cent_pos]).astype(jnp.int32)
    pair_flops = 2 * row_len * SIDE * BLK * width
    factor = 1.0 / width**0.5
    stat_shape = shape((SIDE * SIDE + 2 * SIDE * SIDE, row_len), f32)

    def exp_shapes(values):
        return [shape((BLK, value.shape[0]), f32) for value in values for _ in range(SIDE)]

    *near_exps, near_stats = call(
        functools.partial(near_score_kernel, factor),
        exp_shapes(near) + [stat_shape],
        2 + len(near) + SIDE,
        16,
        flops=3 * pair_flops,
        nbytes=14 << 20,
        smem=2,
    )(pos, candidates, *near, *cents)
    *far_exps, own_stats = call(
        functools.partial(far_score_kernel, factor),
        exp_shapes(far) + [stat_shape],
        len(far) + SIDE + 1,
        12,
        flops=pair_flops,
        nbytes=6 << 20,
    )(*far, *cents, near_stats)
    exps = near_exps + far_exps
    all_stats = lax.all_gather(own_stats, AXES, axis_index_groups=row_lines(planes))
    n_cover = planes * CORES * SIDE
    total, *sent, counts, log_rows, line_sum = call(
        sums_kernel,
        [shape((BLK, width), f32)]
        + [shape((BLK, width + PAD), bf16)] * (SIDE - 1)
        + [shape((BLK, PAD), f32), shape((1, row_len), f32), shape((n_cover, PAD), f32)],
        3 + len(exps) + len(rows),
        24,
        flops=SIDE * pair_flops,
        nbytes=16 << 20,
        smem=1,
        scratch=[pltpu.VMEM((SIDE * SIDE, row_len), f32)],
    )(row_pos.reshape(1).astype(jnp.int32), all_stats, own_stats, *exps, *rows)
    line_sum, total = lax.optimization_barrier((line_sum, total))
    cover_sums = lax.all_to_all(
        line_sum, AXES, 0, 0, tiled=True, axis_index_groups=line_covers(planes)
    )
    received = [bulk(sent[j - 1], cent_pairs(planes, SHIFTS[j])) for j in (3, 2, 1)]
    tile = BLK // 2
    spec = lambda cols: pl.BlockSpec((tile, cols), lambda i: (i, 0))
    new_centroids = pl.pallas_call(
        final_kernel,
        name="final",
        grid=(BLK // tile,),
        out_shape=shape((BLK, width), f32),
        in_specs=[spec(width), spec(PAD)] + [spec(width + PAD)] * 3 + [spec(width)],
        out_specs=spec(width),
        cost_estimate=pl.CostEstimate(flops=0, bytes_accessed=5 << 20, transcendentals=0),
        compiler_params=pltpu.CompilerParams(vmem_limit_bytes=8 << 20),
    )(total, counts, *received, centroids)
    n_rows = row_len * lax.axis_size("dp") * SIDE * SIDE
    new_centroids, cover_sums = lax.optimization_barrier((new_centroids, cover_sums))
    objective = jnp.sum(cover_sums[:, 0]) / n_rows
    return new_centroids, log_rows.reshape(row_len), objective


def solution(mesh):
    in_specs = (P(AXES, None), P(AXES, None), P(AXES, None))
    out_specs = (P(AXES, None), P(AXES), P())
    return jax.shard_map(step, mesh=mesh, in_specs=in_specs, out_specs=out_specs, check_vma=False)
```
